32 devices in a mesh: grp: 2 (over x), had: 16 (over z, y, core).
Axes of the slice: x: 2, y: 2, z: 4, core: 2. Of those that a mesh axis runs over, the one named last changes fastest.
Arguments:
- source_slabs: bfloat16 [512, 128, 128], P(('grp', 'had')), parts along dimension 0, may hold values from -6 to 6
- sink_slabs: bfloat16 [512, 128, 128], P(('grp', 'had')), parts along dimension 0, may hold values from -6 to 6
- perambulators: bfloat16 [4, 2, 128, 128], P('grp'), parts along dimension 0, may hold values from -0.5 to 0.5
- send_pick: int32 [32, 16], P(('grp', 'had')), parts along dimension 0, may hold values from 0 to 15
- graph_slot: int32 [32, 512, 2], P(('grp', 'had')), parts along dimension 0, may hold values from 0 to 15
- graph_sink: int32 [32, 512, 2], P(('grp', 'had')), parts along dimension 0, may hold values from 0 to 15
- graph_count: int32 [32], P(('grp', 'had')), parts along dimension 0, may hold values from 64 to 512, as said below
- pair_list: int32 [256, 2], P(('grp', 'had')), parts along dimension 0, may hold values from 0 to 15
Outputs:
- edge_matrices: bfloat16 [32, 128, 128], P(('grp', 'had')), parts along dimension 0
- pair_products: bfloat16 [256, 128, 128], P(('grp', 'had')), parts along dimension 0
The draws below stay inside these ranges and needn't reach their ends.
There are 2 independent parts, one for each index of `grp`. The reference program is written for one: setup_inputs(seed, part) draws one part's arguments, and reference() takes and returns one part's arrays. A program takes and returns all parts, laid end to end along the dimension named above; each array names one. Nothing has to cross between parts.
Inputs may be any that keep to these rules, and one draw needn't show every extreme that they name: Some reader uses all 512 graph slots; slots from graph_count on are unused.
All inputs are finite; a program needn't handle non-finite values.
Results may differ from the reference program's by a relative error of at most 0.012.
Values may be sent and summed in bfloat16 or wider, within the bound.
A program may use at most 64 MiB of HBM per device.

```python
import math
import jax
import jax.numpy as jnp
from jax import lax

EVECS = 128
SLAB_DEV = 16
GRAPH_DEV = 512
READERS = 16
SLABS = 256
TSLICES = 2
PAIRS = 128


def draw_graph_count(key, part):
    shift_key, top_key = jax.random.split(jax.random.fold_in(key, 17))
    levels = jnp.array([GRAPH_DEV, GRAPH_DEV // 2, GRAPH_DEV // 4, GRAPH_DEV // 8], dtype=jnp.int32)
    chosen = levels[jax.random.randint(shift_key, (READERS,), 0, 4)]
    busiest = jax.random.randint(top_key, (), 0, READERS)
    return jnp.where(jnp.arange(READERS) == busiest, GRAPH_DEV, chosen).astype(jnp.int32)


def with_ends(drawn, own_key, smallest, top_value):
    dims = drawn.shape
    place = [jax.random.randint(jax.random.fold_in(own_key, axis), (), 0, dims[axis]) for axis in range(len(dims))]
    drawn = drawn.at[tuple(place)].set(smallest)
    longest = dims.index(max(dims))
    place[longest] = (place[longest] + 1) % dims[longest]
    return drawn.at[tuple(place)].set(top_value)


def block_scale(key, shape, cuts, least, top_value):
    gain = 1.0
    for position, shards_of in cuts:
        heights = jax.random.uniform(jax.random.fold_in(jax.random.fold_in(key, 6), position), (shards_of,), jnp.float32, least / len(cuts), top_value / len(cuts))
        gain = gain * jnp.repeat(jnp.exp(heights), shape[position] // shards_of).reshape((-1,) + (1,) * (len(shape) - 1 - position))
    return gain


def centred(own_key, dims, width, limit, shards=(), kind=jnp.bfloat16):
    level = block_scale(own_key, dims, shards, -0.22, 0.18) if shards else 1.0
    values = jax.random.normal(own_key, dims, jnp.float32) * width * level
    return jnp.minimum(jnp.maximum(values, -limit), limit).astype(kind)


def setup_inputs(seed: int = 0, part: int = 0) -> dict:
    key_of = jax.random.split(jax.random.key(seed), 9)
    part_splits = jax.random.split(jax.random.fold_in(key_of[8], part), 9)
    source_slabs = centred(part_splits[0], (SLABS, EVECS, EVECS), 1.0, 6.0, ((0, 16),))
    sink_slabs = centred(part_splits[1], (SLABS, EVECS, EVECS), 1.0, 6.0, ((0, 16),))
    perambulators = centred(part_splits[2], (TSLICES, 2, EVECS, EVECS), EVECS ** -0.5, 0.5)
    send_pick = with_ends(jax.random.randint(part_splits[3], (READERS, READERS), 0, SLAB_DEV), jax.random.fold_in(part_splits[3], 1), 0, SLAB_DEV - 1).astype(jnp.int32)
    graph_slot = with_ends(jax.random.randint(part_splits[4], (READERS, GRAPH_DEV, 2), 0, READERS), jax.random.fold_in(part_splits[4], 1), 0, READERS - 1).astype(jnp.int32)
    graph_sink = with_ends(jax.random.randint(part_splits[5], (READERS, GRAPH_DEV, 2), 0, SLAB_DEV), jax.random.fold_in(part_splits[5], 1), 0, SLAB_DEV - 1).astype(jnp.int32)
    graph_count = draw_graph_count(jax.random.fold_in(jax.random.fold_in(key_of[8], part), 71), part)
    pair_list = with_ends(jax.random.randint(part_splits[7], (PAIRS, 2), 0, READERS), jax.random.fold_in(part_splits[7], 1), 0, READERS - 1).astype(jnp.int32)
    return dict(source_slabs=source_slabs, sink_slabs=sink_slabs, perambulators=perambulators, send_pick=send_pick, graph_slot=graph_slot, graph_sink=graph_sink, graph_count=graph_count, pair_list=pair_list)


def rotated_slabs(source_slabs, perambulators):
    grouped = source_slabs.reshape(TSLICES, EVECS, EVECS, EVECS).astype(jnp.float32)
    first_turn = jnp.einsum('txa,tcab->tcxb', perambulators[:, 0].astype(jnp.float32), grouped).astype(jnp.bfloat16)
    second_turn = jnp.einsum('tcxb,tyb->tcxy', first_turn.astype(jnp.float32), perambulators[:, 1].astype(jnp.float32))
    return second_turn.astype(jnp.bfloat16).reshape(SLABS, EVECS, EVECS)

def reference(source_slabs, sink_slabs, perambulators, send_pick, graph_slot, graph_sink, graph_count, pair_list):
    rotated = rotated_slabs(source_slabs, perambulators)
    root_scale = 1.0 / math.sqrt(EVECS)
    edge_scale = 1.0 / math.sqrt(EVECS * GRAPH_DEV)
    owners = jnp.arange(READERS, dtype=jnp.int32)

    def reader_edge(packed):
        reader, slot_rows, sink_rows, graph_total = packed
        pick_column = lax.dynamic_index_in_dim(send_pick, reader, 1, keepdims=False)
        received = rotated[(owners * SLAB_DEV + pick_column).astype(jnp.int32)]
        resident = lax.dynamic_slice_in_dim(sink_slabs, (reader * SLAB_DEV).astype(jnp.int32), SLAB_DEV, 0)

        def factor(slots, sinks):
            product = jnp.einsum('gxb,gab->gxa', resident[sinks].astype(jnp.float32), received[slots].astype(jnp.float32))
            return (product * root_scale).astype(jnp.bfloat16)
        is_valid = (jnp.arange(GRAPH_DEV, dtype=jnp.int32) < graph_total).astype(jnp.float32)
        left_side = factor(slot_rows[:, 0], sink_rows[:, 0]).astype(jnp.float32) * is_valid[:, None, None]
        right_side = factor(slot_rows[:, 1], sink_rows[:, 1]).astype(jnp.float32)
        summed = jnp.einsum('gxa,gay->xy', left_side, right_side)
        return (summed * edge_scale).astype(jnp.bfloat16)
    edge_matrices = lax.map(reader_edge, (owners, graph_slot, graph_sink, graph_count))
    left_edges = edge_matrices[pair_list[:, 0]].astype(jnp.float32)
    right_edges = edge_matrices[pair_list[:, 1]].astype(jnp.float32)
    pair_products = (jnp.einsum('pxa,pay->pxy', left_edges, right_edges) * root_scale).astype(jnp.bfloat16)
    return (edge_matrices, pair_products)
```

```python
import functools
import math

import jax
import jax.numpy as jnp
from jax import lax
from jax.experimental import pallas as pl
from jax.experimental.pallas import tpu as pltpu
from jax.sharding import PartitionSpec as P


def looped_shards(
    source_slabs,
    sink_slabs,
    perambulators,
    send_pick,
    graph_slot,
    graph_sink,
    graph_count,
    pair_list,
):
    my_index = lax.axis_index("had")
    evecs = source_slabs.shape[1]
    per_device = source_slabs.shape[0]
    root_scale = 1.0 / math.sqrt(evecs)
    edge_scale = 1.0 / math.sqrt(evecs * graph_slot.shape[1])
    timeslice = my_index * per_device // evecs
    local_peram = lax.dynamic_index_in_dim(perambulators, timeslice, 0, keepdims=False)
    first_turn = jnp.einsum(
        "xa,jab->xjb", local_peram[0], source_slabs, preferred_element_type=jnp.float32
    ).astype(jnp.bfloat16)
    pick_row = send_pick[0]
    second_turn = jnp.einsum(
        "xjb,yb->xjy", first_turn, local_peram[1], preferred_element_type=jnp.float32
    ).astype(jnp.bfloat16)
    outgoing = jnp.take(second_turn, pick_row, axis=1)
    received = lax.all_to_all(outgoing, "had", split_axis=1, concat_axis=1, tiled=True)
    graph_rows = graph_slot.shape[1]
    block_width = min(64, graph_rows)
    slot_table = graph_slot[0]
    sink_table = graph_sink[0]
    graph_total = graph_count[0]

    def factor(slots, sinks):
        gathered = jnp.take(received, slots, axis=1)
        resident = jnp.take(sink_slabs, sinks, axis=0)
        product = jnp.einsum("gxb,agb->gxa", resident, gathered, preferred_element_type=jnp.float32)
        return (product * root_scale).astype(jnp.bfloat16)

    def accumulate(block_index, running_sum):
        offset = block_index * block_width
        slots = lax.dynamic_slice_in_dim(slot_table, offset, block_width, 0)
        sinks = lax.dynamic_slice_in_dim(sink_table, offset, block_width, 0)
        is_valid = (offset + jnp.arange(block_width, dtype=jnp.int32) < graph_total).astype(
            jnp.bfloat16
        )
        left_side = factor(slots[:, 0], sinks[:, 0]) * is_valid[:, None, None]
        right_side = factor(slots[:, 1], sinks[:, 1])
        return running_sum + jnp.einsum(
            "gxa,gay->xy", left_side, right_side, preferred_element_type=jnp.float32
        )

    block_count = (graph_total + block_width - 1) // block_width
    summed = lax.fori_loop(0, block_count, accumulate, jnp.zeros((evecs, evecs), jnp.float32))
    edge_local = (summed * edge_scale).astype(jnp.bfloat16)[None]
    left_ids = pair_list[:, 0]
    right_ids = pair_list[:, 1]
    shard_rows = lax.all_gather(edge_local, "had", axis=0, tiled=True)
    row_ids = jnp.arange(shard_rows.shape[0], dtype=jnp.int32)
    left_select = (left_ids[:, None] == row_ids[None, :]).astype(jnp.bfloat16)
    right_select = (right_ids[:, None] == row_ids[None, :]).astype(jnp.bfloat16)
    left_part = jnp.einsum(
        "pn,nxy->pxy", left_select, shard_rows, preferred_element_type=jnp.float32
    )
    right_part = jnp.einsum(
        "pn,nxy->pxy", right_select, shard_rows, preferred_element_type=jnp.float32
    )
    left_edges = left_part.astype(jnp.bfloat16)
    right_edges = right_part.astype(jnp.bfloat16)
    product = jnp.einsum(
        "pxa,pay->pxy", left_edges, right_edges, preferred_element_type=jnp.float32
    )
    pair_products = (product * root_scale).astype(jnp.bfloat16)
    return (edge_local, pair_products)


NT = (((1,), (1,)), ((), ()))
UNROLL = 8


def flip(index, step):
    flipped = index
    bit = 1
    while bit <= step:
        if step & bit:
            flipped = flipped + bit * (1 - 2 * (index // bit % 2))
        bit *= 2
    return flipped


def fused_kernel(
    n,
    graphs,
    pick_ref,
    slot_ref,
    graph_sink_ref,
    count_ref,
    pair_ref,
    peram_ref,
    source_ref,
    sink_ref,
    edge_ref,
    product_ref,
    outgoing,
    received,
    table,
    edges,
    graph_ref,
    send_sem,
    recv_sem,
    edge_send_sem,
    edge_recv_sem,
):
    me = lax.axis_index("had")
    per_device, evecs, _ = source_ref.shape
    root_scale = 1.0 / math.sqrt(evecs)
    edge_scale = 1.0 / math.sqrt(evecs * graphs)
    sinks = sink_ref.shape[0]

    def at(peer):
        return dict(device_id={"had": peer}, device_id_type=pl.DeviceIdType.MESH)

    barrier = pltpu.get_barrier_semaphore()
    for step in range(1, n):
        pl.semaphore_signal(barrier, inc=1, **at(flip(me, step)))

    timeslice = me * per_device // evecs
    first = peram_ref[timeslice, 0]
    second = peram_ref[timeslice, 1]

    def rotate(reader):
        slab = source_ref[pick_ref[0, reader]]
        half = jnp.dot(first, slab, preferred_element_type=jnp.float32).astype(jnp.bfloat16)
        turned = lax.dot_general(half, second, NT, preferred_element_type=jnp.float32)
        return turned.astype(jnp.bfloat16)

    def rotate_step(reader, carry):
        outgoing[reader] = rotate(reader)
        return carry

    lax.fori_loop(0, n, rotate_step, 0, unroll=4)
    received[me] = outgoing[me]
    pl.semaphore_wait(barrier, n - 1)

    order = list(range(n - 1, 0, -1))
    copies = []
    for step in order:
        peer = flip(me, step)
        copy = pltpu.make_async_remote_copy(
            src_ref=outgoing.at[peer],
            dst_ref=received.at[me],
            send_sem=send_sem.at[step],
            recv_sem=recv_sem.at[step],
            **at(peer),
        )
        copy.start()
        copies.append(copy)

    def index_step(graph, carry):
        for side in range(2):
            index = slot_ref[side, graph] * sinks + graph_sink_ref[side, graph]
            graph_ref[2 * graph + side] = jnp.where(graph < count_ref[0], index, n * sinks)
        return carry

    lax.fori_loop(0, graphs, index_step, 0, unroll=4)
    table[n * sinks] = jnp.zeros((evecs, evecs), jnp.bfloat16)
    rows = 4

    for chip in range(n // 2):
        for core in range(2):
            step = 2 * chip + core
            if step:
                copies[order.index(step)].wait_recv()
        base = (flip(me, 2 * chip)) // 2 * 2
        both = received[pl.ds(base, 2)].reshape(2 * evecs, evecs)
        for block in range(sinks // rows):
            left = sink_ref[block * rows : (block + 1) * rows].reshape(rows * evecs, evecs)
            product = lax.dot_general(left, both, NT, preferred_element_type=jnp.float32)
            scaled = (product * root_scale).astype(jnp.bfloat16)
            for core in range(2):
                part = scaled[:, core * evecs : (core + 1) * evecs].reshape(rows, evecs, evecs)
                table[pl.ds((base + core) * sinks + block * rows, rows)] = part
    for copy in copies:
        copy.wait_send()

    def graph_step(block, total):
        for inner in range(0, UNROLL, 2):
            index = 2 * (block * UNROLL + inner)
            left = jnp.concatenate([table[graph_ref[index]], table[graph_ref[index + 2]]], axis=1)
            right = jnp.concatenate(
                [table[graph_ref[index + 1]], table[graph_ref[index + 3]]], axis=0
            )
            total = total + jnp.dot(left, right, preferred_element_type=jnp.float32)
        return total

    total = lax.fori_loop(
        0, graphs // UNROLL, graph_step, jnp.zeros((evecs, evecs), jnp.float32)
    )
    edge = (total * edge_scale).astype(jnp.bfloat16)
    edge_ref[0] = edge
    edges[me] = edge

    sent = []

    def pass_on(step, peer_step, kind):
        owner = flip(me, step)
        slot = step if kind else peer_step
        copy = pltpu.make_async_remote_copy(
            src_ref=edges.at[owner],
            dst_ref=edges.at[owner],
            send_sem=edge_send_sem.at[kind, slot],
            recv_sem=edge_recv_sem.at[step ^ peer_step],
            **at(flip(me, peer_step)),
        )
        copy.start()
        sent.append(copy)

    def arrived(step):
        pltpu.make_async_remote_copy(
            src_ref=edges.at[me],
            dst_ref=edges.at[flip(me, step)],
            send_sem=edge_send_sem.at[0, 0],
            recv_sem=edge_recv_sem.at[step],
            **at(flip(me, 1)),
        ).wait_recv()

    for step in range(n - 4, 0, -4):
        pass_on(0, step, 0)
    pass_on(0, 2, 1)
    pass_on(0, 1, 2)
    for step in range(4, n, 4):
        arrived(step)
        pass_on(step, 2, 1)
        pass_on(step, 1, 2)
    for step in range(2, n, 4):
        arrived(step)
        pass_on(step, 1, 2)
    for step in range(1, n, 2):
        arrived(step)
    for copy in sent:
        copy.wait_send()

    for pair in range(product_ref.shape[0]):
        product = jnp.dot(
            edges[pair_ref[0, pair]],
            edges[pair_ref[1, pair]],
            preferred_element_type=jnp.float32,
        )
        product_ref[pair] = (product * root_scale).astype(jnp.bfloat16)


def fused_shards(
    n,
    source_slabs,
    sink_slabs,
    perambulators,
    send_pick,
    graph_slot,
    graph_sink,
    graph_count,
    pair_list,
):
    sinks, evecs, _ = sink_slabs.shape
    graphs = graph_slot.shape[1]
    vmem = pl.BlockSpec(memory_space=pltpu.VMEM)
    smem = pl.BlockSpec(memory_space=pltpu.SMEM)
    slab = (evecs, evecs)
    return pl.pallas_call(
        functools.partial(fused_kernel, n, graphs),
        out_shape=(
            jax.ShapeDtypeStruct((1, *slab), jnp.bfloat16),
            jax.ShapeDtypeStruct((pair_list.shape[0], *slab), jnp.bfloat16),
        ),
        in_specs=[smem, smem, smem, smem, smem, vmem, vmem, vmem],
        out_specs=(vmem, vmem),
        scratch_shapes=[
            pltpu.VMEM((n, *slab), jnp.bfloat16),
            pltpu.VMEM((n, *slab), jnp.bfloat16),
            pltpu.VMEM((n * sinks + 1, *slab), jnp.bfloat16),
            pltpu.VMEM((n, *slab), jnp.bfloat16),
            pltpu.SMEM((2 * graphs,), jnp.int32),
            pltpu.SemaphoreType.DMA((n,)),
            pltpu.SemaphoreType.DMA((n,)),
            pltpu.SemaphoreType.DMA((3, n)),
            pltpu.SemaphoreType.DMA((n,)),
        ],
        compiler_params=pltpu.CompilerParams(collective_id=0, has_side_effects=True),
        name="contraction",
    )(
        send_pick,
        graph_slot[0].T,
        graph_sink[0].T,
        graph_count,
        pair_list.T,
        perambulators,
        source_slabs,
        sink_slabs,
    )


def shards(readers, source_slabs, sink_slabs, perambulators, *tables):
    slabs = sink_slabs.shape[0]
    graphs = tables[1].shape[1]
    power = readers & (readers - 1) == 0 and readers % 4 == 0
    if power and readers * slabs <= 2 * graphs and graphs % UNROLL == 0 and slabs % 4 == 0:
        return fused_shards(readers, source_slabs, sink_slabs, perambulators, *tables)
    return looped_shards(source_slabs, sink_slabs, perambulators, *tables)


def solution(mesh):
    return jax.shard_map(
        functools.partial(shards, mesh.shape["had"]),
        mesh=mesh,
        in_specs=(
            P(("grp", "had"), None, None),
            P(("grp", "had"), None, None),
            P("grp", None, None, None),
            P(("grp", "had"), None),
            P(("grp", "had"), None, None),
            P(("grp", "had"), None, None),
            P(("grp", "had")),
            P(("grp", "had"), None),
        ),
        out_specs=(P(("grp", "had"), None, None), P(("grp", "had"), None, None)),
        check_vma=False,
    )
```

```python
import functools
import math

import jax
import jax.numpy as jnp
from jax import lax
from jax.experimental import pallas as pl
from jax.experimental.pallas import tpu as pltpu
from jax.sharding import PartitionSpec as P


def looped_shards(
    source_slabs,
    sink_slabs,
    perambulators,
    send_pick,
    graph_slot,
    graph_sink,
    graph_count,
    pair_list,
):
    my_index = lax.axis_index("had")
    evecs = source_slabs.shape[1]
    per_device = source_slabs.shape[0]
    root_scale = 1.0 / math.sqrt(evecs)
    edge_scale = 1.0 / math.sqrt(evecs * graph_slot.shape[1])
    timeslice = my_index * per_device // evecs
    local_peram = lax.dynamic_index_in_dim(perambulators, timeslice, 0, keepdims=False)
    first_turn = jnp.einsum(
        "xa,jab->xjb", local_peram[0], source_slabs, preferred_element_type=jnp.float32
    ).astype(jnp.bfloat16)
    pick_row = send_pick[0]
    second_turn = jnp.einsum(
        "xjb,yb->xjy", first_turn, local_peram[1], preferred_element_type=jnp.float32
    ).astype(jnp.bfloat16)
    outgoing = jnp.take(second_turn, pick_row, axis=1)
    received = lax.all_to_all(outgoing, "had", split_axis=1, concat_axis=1, tiled=True)
    graph_rows = graph_slot.shape[1]
    block_width = min(64, graph_rows)
    slot_table = graph_slot[0]
    sink_table = graph_sink[0]
    graph_total = graph_count[0]

    def factor(slots, sinks):
        gathered = jnp.take(received, slots, axis=1)
        resident = jnp.take(sink_slabs, sinks, axis=0)
        product = jnp.einsum("gxb,agb->gxa", resident, gathered, preferred_element_type=jnp.float32)
        return (product * root_scale).astype(jnp.bfloat16)

    def accumulate(block_index, running_sum):
        offset = block_index * block_width
        slots = lax.dynamic_slice_in_dim(slot_table, offset, block_width, 0)
        sinks = lax.dynamic_slice_in_dim(sink_table, offset, block_width, 0)
        is_valid = (offset + jnp.arange(block_width, dtype=jnp.int32) < graph_total).astype(
            jnp.bfloat16
        )
        left_side = factor(slots[:, 0], sinks[:, 0]) * is_valid[:, None, None]
        right_side = factor(slots[:, 1], sinks[:, 1])
        return running_sum + jnp.einsum(
            "gxa,gay->xy", left_side, right_side, preferred_element_type=jnp.float32
        )

    block_count = (graph_total + block_width - 1) // block_width
    summed = lax.fori_loop(0, block_count, accumulate, jnp.zeros((evecs, evecs), jnp.float32))
    edge_local = (summed * edge_scale).astype(jnp.bfloat16)[None]
    left_ids = pair_list[:, 0]
    right_ids = pair_list[:, 1]
    shard_rows = lax.all_gather(edge_local, "had", axis=0, tiled=True)
    row_ids = jnp.arange(shard_rows.shape[0], dtype=jnp.int32)
    left_select = (left_ids[:, None] == row_ids[None, :]).astype(jnp.bfloat16)
    right_select = (right_ids[:, None] == row_ids[None, :]).astype(jnp.bfloat16)
    left_part = jnp.einsum(
        "pn,nxy->pxy", left_select, shard_rows, preferred_element_type=jnp.float32
    )
    right_part = jnp.einsum(
        "pn,nxy->pxy", right_select, shard_rows, preferred_element_type=jnp.float32
    )
    left_edges = left_part.astype(jnp.bfloat16)
    right_edges = right_part.astype(jnp.bfloat16)
    product = jnp.einsum(
        "pxa,pay->pxy", left_edges, right_edges, preferred_element_type=jnp.float32
    )
    pair_products = (product * root_scale).astype(jnp.bfloat16)
    return (edge_local, pair_products)


NT = (((1,), (1,)), ((), ()))
UNROLL = 128


def flip(index, step):
    flipped = index
    bit = 1
    while bit <= step:
        if step & bit:
            flipped = flipped + bit * (1 - 2 * (index // bit % 2))
        bit *= 2
    return flipped


def fused_kernel(
    n,
    graphs,
    pick_ref,
    slot_ref,
    graph_sink_ref,
    count_ref,
    peram_in,
    source_in,
    sink_in,
    edges,
    outgoing,
    received,
    table,
    graph_ref,
    peram_ref,
    source_ref,
    sink_ref,
    load_sem,
    send_sem,
    recv_sem,
    edge_send_sem,
    edge_recv_sem,
):
    me = lax.axis_index("had")
    per_device, evecs, _ = source_ref.shape
    root_scale = 1.0 / math.sqrt(evecs)
    edge_scale = 1.0 / math.sqrt(evecs * graphs)
    sinks = sink_ref.shape[0]

    def at(peer):
        return dict(device_id={"had": peer}, device_id_type=pl.DeviceIdType.MESH)

    barrier = pltpu.get_barrier_semaphore()
    for step in range(1, n):
        pl.semaphore_signal(barrier, inc=1, **at(flip(me, step)))

    peram_load = pltpu.make_async_copy(peram_in, peram_ref, load_sem.at[0])
    source_load = pltpu.make_async_copy(source_in, source_ref, load_sem.at[1])
    sink_load = pltpu.make_async_copy(sink_in, sink_ref, load_sem.at[2])
    peram_load.start()
    source_load.start()
    sink_load.start()
    peram_load.wait()
    source_load.wait()

    timeslice = me * per_device // evecs
    first = peram_ref[timeslice, 0]
    second = peram_ref[timeslice, 1]

    def rotate(reader):
        slab = source_ref[pick_ref[0, reader]]
        half = jnp.dot(first, slab, preferred_element_type=jnp.float32).astype(jnp.bfloat16)
        turned = lax.dot_general(half, second, NT, preferred_element_type=jnp.float32)
        return turned.astype(jnp.bfloat16)

    def rotate_step(reader, carry):
        outgoing[reader] = rotate(reader)
        return carry

    lax.fori_loop(0, n, rotate_step, 0, unroll=4)
    received[me] = outgoing[me]
    pl.semaphore_wait(barrier, n - 1)

    order = list(range(1, n))
    copies = []
    for step in order:
        peer = flip(me, step)
        copy = pltpu.make_async_remote_copy(
            src_ref=outgoing.at[peer],
            dst_ref=received.at[me],
            send_sem=send_sem.at[step],
            recv_sem=recv_sem.at[step],
            **at(peer),
        )
        copy.start()
        copies.append(copy)

    def index_step(graph, carry):
        for side in range(2):
            index = slot_ref[side, graph] * sinks + graph_sink_ref[side, graph]
            graph_ref[2 * graph + side] = jnp.where(graph < count_ref[0], index, n * sinks)
        return carry

    lax.fori_loop(0, graphs, index_step, 0, unroll=4)
    table[n * sinks] = jnp.zeros((evecs, evecs), jnp.bfloat16)
    rows = 4
    sink_load.wait()

    for chip in range(n // 2):
        for core in range(2):
            step = 2 * chip + core
            if step:
                copies[order.index(step)].wait_recv()
        base = (flip(me, 2 * chip)) // 2 * 2
        both = received[pl.ds(base, 2)].reshape(2 * evecs, evecs)
        for block in range(sinks // rows):
            left = sink_ref[block * rows : (block + 1) * rows].reshape(rows * evecs, evecs)
            product = lax.dot_general(left, both, NT, preferred_element_type=jnp.float32)
            scaled = (product * root_scale).astype(jnp.bfloat16)
            for core in range(2):
                part = scaled[:, core * evecs : (core + 1) * evecs].reshape(rows, evecs, evecs)
                table[pl.ds((base + core) * sinks + block * rows, rows)] = part
    for copy in copies:
        copy.wait_send()

    def graph_step(block, total):
        first = 2 * UNROLL * block
        left = [table[graph_ref[first + 2 * graph]] for graph in range(UNROLL)]
        right = [table[graph_ref[first + 2 * graph + 1]] for graph in range(UNROLL)]
        return total + jnp.dot(
            jnp.concatenate(left, axis=1),
            jnp.concatenate(right, axis=0),
            preferred_element_type=jnp.float32,
        )

    total = lax.fori_loop(
        0, graphs // UNROLL, graph_step, jnp.zeros((evecs, evecs), jnp.float32)
    )
    edge = (total * edge_scale).astype(jnp.bfloat16)
    edges[me] = edge

    sent = []

    def pass_on(step, peer_step, kind):
        owner = flip(me, step)
        slot = step if kind else peer_step
        copy = pltpu.make_async_remote_copy(
            src_ref=edges.at[owner],
            dst_ref=edges.at[owner],
            send_sem=edge_send_sem.at[kind, slot],
            recv_sem=edge_recv_sem.at[step ^ peer_step],
            **at(flip(me, peer_step)),
        )
        copy.start()
        sent.append(copy)

    def arrived(step):
        pltpu.make_async_remote_copy(
            src_ref=edges.at[me],
            dst_ref=edges.at[flip(me, step)],
            send_sem=edge_send_sem.at[0, 0],
            recv_sem=edge_recv_sem.at[step],
            **at(flip(me, 1)),
        ).wait_recv()

    for step in range(n - 4, 0, -4):
        pass_on(0, step, 0)
    pass_on(0, 2, 1)
    pass_on(0, 1, 2)
    for step in range(4, n, 4):
        arrived(step)
        pass_on(step, 2, 1)
        pass_on(step, 1, 2)
    for step in range(2, n, 4):
        arrived(step)
        pass_on(step, 1, 2)
    for step in range(1, n, 2):
        arrived(step)
    for copy in sent:
        copy.wait_send()


def pair_kernel(pair_ref, edges, edge_ref, product_ref):
    me = lax.axis_index("had")
    root_scale = 1.0 / math.sqrt(edges.shape[1])
    edge_ref[0] = edges[me]
    for pair in range(product_ref.shape[0]):
        product = jnp.dot(
            edges[pair_ref[0, pair]],
            edges[pair_ref[1, pair]],
            preferred_element_type=jnp.float32,
        )
        product_ref[pair] = (product * root_scale).astype(jnp.bfloat16)


def fused_shards(
    n,
    source_slabs,
    sink_slabs,
    perambulators,
    send_pick,
    graph_slot,
    graph_sink,
    graph_count,
    pair_list,
):
    sinks, evecs, _ = sink_slabs.shape
    graphs = graph_slot.shape[1]
    vmem = pl.BlockSpec(memory_space=pltpu.VMEM)
    hbm = pl.BlockSpec(memory_space=pl.ANY)
    smem = pl.BlockSpec(memory_space=pltpu.SMEM)
    slab = (evecs, evecs)
    edges = pl.pallas_call(
        functools.partial(fused_kernel, n, graphs),
        out_shape=jax.ShapeDtypeStruct((n, *slab), jnp.bfloat16),
        in_specs=[smem, smem, smem, smem, hbm, hbm, hbm],
        out_specs=vmem,
        scratch_shapes=[
            pltpu.VMEM((n, *slab), jnp.bfloat16),
            pltpu.VMEM((n, *slab), jnp.bfloat16),
            pltpu.VMEM((n * sinks + 1, *slab), jnp.bfloat16),
            pltpu.SMEM((2 * graphs,), jnp.int32),
            pltpu.VMEM(perambulators.shape, jnp.bfloat16),
            pltpu.VMEM(source_slabs.shape, jnp.bfloat16),
            pltpu.VMEM(sink_slabs.shape, jnp.bfloat16),
            pltpu.SemaphoreType.DMA((3,)),
            pltpu.SemaphoreType.DMA((n,)),
            pltpu.SemaphoreType.DMA((n,)),
            pltpu.SemaphoreType.DMA((3, n)),
            pltpu.SemaphoreType.DMA((n,)),
        ],
        compiler_params=pltpu.CompilerParams(collective_id=0, has_side_effects=True),
        name="contraction",
    )(
        send_pick,
        graph_slot[0].T,
        graph_sink[0].T,
        graph_count,
        perambulators,
        source_slabs,
        sink_slabs,
    )
    return pl.pallas_call(
        pair_kernel,
        out_shape=(
            jax.ShapeDtypeStruct((1, *slab), jnp.bfloat16),
            jax.ShapeDtypeStruct((pair_list.shape[0], *slab), jnp.bfloat16),
        ),
        in_specs=[smem, vmem],
        out_specs=(vmem, vmem),
        name="pairs",
    )(pair_list.T, edges)


def shards(readers, source_slabs, sink_slabs, perambulators, *tables):
    slabs = sink_slabs.shape[0]
    graphs = tables[1].shape[1]
    power = readers & (readers - 1) == 0 and readers % 4 == 0
    if power and readers * slabs <= 2 * graphs and graphs % UNROLL == 0 and slabs % 4 == 0:
        return fused_shards(readers, source_slabs, sink_slabs, perambulators, *tables)
    return looped_shards(source_slabs, sink_slabs, perambulators, *tables)


def solution(mesh):
    return jax.shard_map(
        functools.partial(shards, mesh.shape["had"]),
        mesh=mesh,
        in_specs=(
            P(("grp", "had"), None, None),
            P(("grp", "had"), None, None),
            P("grp", None, None, None),
            P(("grp", "had"), None),
            P(("grp", "had"), None, None),
            P(("grp", "had"), None, None),
            P(("grp", "had")),
            P(("grp", "had"), None),
        ),
        out_specs=(P(("grp", "had"), None, None), P(("grp", "had"), None, None)),
        check_vma=False,
    )
```

```python
import functools
import math

import jax
import jax.numpy as jnp
from jax import lax
from jax.experimental import pallas as pl
from jax.experimental.pallas import tpu as pltpu
from jax.sharding import PartitionSpec as P


def looped_shards(
    source_slabs,
    sink_slabs,
    perambulators,
    send_pick,
    graph_slot,
    graph_sink,
    graph_count,
    pair_list,
):
    my_index = lax.axis_index("had")
    evecs = source_slabs.shape[1]
    per_device = source_slabs.shape[0]
    root_scale = 1.0 / math.sqrt(evecs)
    edge_scale = 1.0 / math.sqrt(evecs * graph_slot.shape[1])
    timeslice = my_index * per_device // evecs
    local_peram = lax.dynamic_index_in_dim(perambulators, timeslice, 0, keepdims=False)
    first_turn = jnp.einsum(
        "xa,jab->xjb", local_peram[0], source_slabs, preferred_element_type=jnp.float32
    ).astype(jnp.bfloat16)
    pick_row = send_pick[0]
    second_turn = jnp.einsum(
        "xjb,yb->xjy", first_turn, local_peram[1], preferred_element_type=jnp.float32
    ).astype(jnp.bfloat16)
    outgoing = jnp.take(second_turn, pick_row, axis=1)
    received = lax.all_to_all(outgoing, "had", split_axis=1, concat_axis=1, tiled=True)
    graph_rows = graph_slot.shape[1]
    block_width = min(64, graph_rows)
    slot_table = graph_slot[0]
    sink_table = graph_sink[0]
    graph_total = graph_count[0]

    def factor(slots, sinks):
        gathered = jnp.take(received, slots, axis=1)
        resident = jnp.take(sink_slabs, sinks, axis=0)
        product = jnp.einsum("gxb,agb->gxa", resident, gathered, preferred_element_type=jnp.float32)
        return (product * root_scale).astype(jnp.bfloat16)

    def accumulate(block_index, running_sum):
        offset = block_index * block_width
        slots = lax.dynamic_slice_in_dim(slot_table, offset, block_width, 0)
        sinks = lax.dynamic_slice_in_dim(sink_table, offset, block_width, 0)
        is_valid = (offset + jnp.arange(block_width, dtype=jnp.int32) < graph_total).astype(
            jnp.bfloat16
        )
        left_side = factor(slots[:, 0], sinks[:, 0]) * is_valid[:, None, None]
        right_side = factor(slots[:, 1], sinks[:, 1])
        return running_sum + jnp.einsum(
            "gxa,gay->xy", left_side, right_side, preferred_element_type=jnp.float32
        )

    block_count = (graph_total + block_width - 1) // block_width
    summed = lax.fori_loop(0, block_count, accumulate, jnp.zeros((evecs, evecs), jnp.float32))
    edge_local = (summed * edge_scale).astype(jnp.bfloat16)[None]
    left_ids = pair_list[:, 0]
    right_ids = pair_list[:, 1]
    shard_rows = lax.all_gather(edge_local, "had", axis=0, tiled=True)
    row_ids = jnp.arange(shard_rows.shape[0], dtype=jnp.int32)
    left_select = (left_ids[:, None] == row_ids[None, :]).astype(jnp.bfloat16)
    right_select = (right_ids[:, None] == row_ids[None, :]).astype(jnp.bfloat16)
    left_part = jnp.einsum(
        "pn,nxy->pxy", left_select, shard_rows, preferred_element_type=jnp.float32
    )
    right_part = jnp.einsum(
        "pn,nxy->pxy", right_select, shard_rows, preferred_element_type=jnp.float32
    )
    left_edges = left_part.astype(jnp.bfloat16)
    right_edges = right_part.astype(jnp.bfloat16)
    product = jnp.einsum(
        "pxa,pay->pxy", left_edges, right_edges, preferred_element_type=jnp.float32
    )
    pair_products = (product * root_scale).astype(jnp.bfloat16)
    return (edge_local, pair_products)


NT = (((1,), (1,)), ((), ()))
UNROLL = 256


def flip(index, step):
    flipped = index
    bit = 1
    while bit <= step:
        if step & bit:
            flipped = flipped + bit * (1 - 2 * (index // bit % 2))
        bit *= 2
    return flipped


def fused_kernel(
    n,
    graphs,
    pick_ref,
    slot_ref,
    graph_sink_ref,
    count_ref,
    peram_in,
    source_in,
    sink_in,
    edges,
    outgoing,
    received,
    table,
    graph_ref,
    peram_ref,
    source_ref,
    sink_ref,
    load_sem,
    send_sem,
    recv_sem,
    edge_send_sem,
    edge_recv_sem,
):
    me = lax.axis_index("had")
    per_device, evecs, _ = source_ref.shape
    root_scale = 1.0 / math.sqrt(evecs)
    edge_scale = 1.0 / math.sqrt(evecs * graphs)
    sinks = sink_ref.shape[0]

    def at(peer):
        return dict(device_id={"had": peer}, device_id_type=pl.DeviceIdType.MESH)

    barrier = pltpu.get_barrier_semaphore()
    for step in range(1, n):
        pl.semaphore_signal(barrier, inc=1, **at(flip(me, step)))

    peram_load = pltpu.make_async_copy(peram_in, peram_ref, load_sem.at[0])
    source_load = pltpu.make_async_copy(source_in, source_ref, load_sem.at[1])
    sink_load = pltpu.make_async_copy(sink_in, sink_ref, load_sem.at[2])
    peram_load.start()
    source_load.start()
    sink_load.start()
    peram_load.wait()
    source_load.wait()

    timeslice = me * per_device // evecs
    first = peram_ref[timeslice, 0]
    second = peram_ref[timeslice, 1]

    def rotate(reader):
        slab = source_ref[pick_ref[0, reader]]
        half = jnp.dot(first, slab, preferred_element_type=jnp.float32).astype(jnp.bfloat16)
        turned = lax.dot_general(half, second, NT, preferred_element_type=jnp.float32)
        return turned.astype(jnp.bfloat16)

    def rotate_step(reader, carry):
        outgoing[reader] = rotate(reader)
        return carry

    lax.fori_loop(0, n, rotate_step, 0, unroll=4)
    received[me] = outgoing[me]
    pl.semaphore_wait(barrier, n - 1)

    order = list(range(1, n))
    copies = []
    for step in order:
        peer = flip(me, step)
        copy = pltpu.make_async_remote_copy(
            src_ref=outgoing.at[peer],
            dst_ref=received.at[me],
            send_sem=send_sem.at[step],
            recv_sem=recv_sem.at[step],
            **at(peer),
        )
        copy.start()
        copies.append(copy)

    def index_step(graph, carry):
        for side in range(2):
            index = slot_ref[side, graph] * sinks + graph_sink_ref[side, graph]
            graph_ref[2 * graph + side] = jnp.where(graph < count_ref[0], index, n * sinks)
        return carry

    lax.fori_loop(0, graphs, index_step, 0, unroll=4)
    table[n * sinks] = jnp.zeros((evecs, evecs), jnp.bfloat16)
    rows = 4
    sink_load.wait()

    for chip in range(n // 2):
        for core in range(2):
            step = 2 * chip + core
            if step:
                copies[order.index(step)].wait_recv()
        base = (flip(me, 2 * chip)) // 2 * 2
        both = received[pl.ds(base, 2)].reshape(2 * evecs, evecs)
        for block in range(sinks // rows):
            left = sink_ref[block * rows : (block + 1) * rows].reshape(rows * evecs, evecs)
            product = lax.dot_general(left, both, NT, preferred_element_type=jnp.float32)
            scaled = (product * root_scale).astype(jnp.bfloat16)
            for core in range(2):
                part = scaled[:, core * evecs : (core + 1) * evecs].reshape(rows, evecs, evecs)
                table[pl.ds((base + core) * sinks + block * rows, rows)] = part
    for copy in copies:
        copy.wait_send()

    def graph_step(block, total):
        first = 2 * UNROLL * block
        left = [table[graph_ref[first + 2 * graph]] for graph in range(UNROLL)]
        right = [table[graph_ref[first + 2 * graph + 1]] for graph in range(UNROLL)]
        return total + jnp.dot(
            jnp.concatenate(left, axis=1),
            jnp.concatenate(right, axis=0),
            preferred_element_type=jnp.float32,
        )

    total = lax.fori_loop(
        0, graphs // UNROLL, graph_step, jnp.zeros((evecs, evecs), jnp.float32)
    )
    edge = (total * edge_scale).astype(jnp.bfloat16)
    edges[me] = edge

    sent = []

    def pass_on(step, peer_step, kind):
        owner = flip(me, step)
        slot = step if kind else peer_step
        copy = pltpu.make_async_remote_copy(
            src_ref=edges.at[owner],
            dst_ref=edges.at[owner],
            send_sem=edge_send_sem.at[kind, slot],
            recv_sem=edge_recv_sem.at[step ^ peer_step],
            **at(flip(me, peer_step)),
        )
        copy.start()
        sent.append(copy)

    def arrived(step):
        pltpu.make_async_remote_copy(
            src_ref=edges.at[me],
            dst_ref=edges.at[flip(me, step)],
            send_sem=edge_send_sem.at[0, 0],
            recv_sem=edge_recv_sem.at[step],
            **at(flip(me, 1)),
        ).wait_recv()

    for step in range(n - 2, 0, -2):
        pass_on(0, step, 0)
    pass_on(0, 1, 2)
    for step in range(2, n, 2):
        arrived(step)
        pass_on(step, 1, 2)
    for step in range(1, n, 2):
        arrived(step)
    for copy in sent:
        copy.wait_send()


def pair_kernel(pair_ref, edges, edge_ref, product_ref):
    me = lax.axis_index("had")
    root_scale = 1.0 / math.sqrt(edges.shape[1])
    edge_ref[0] = edges[me]
    for pair in range(product_ref.shape[0]):
        product = jnp.dot(
            edges[pair_ref[0, pair]],
            edges[pair_ref[1, pair]],
            preferred_element_type=jnp.float32,
        )
        product_ref[pair] = (product * root_scale).astype(jnp.bfloat16)


def fused_shards(
    n,
    source_slabs,
    sink_slabs,
    perambulators,
    send_pick,
    graph_slot,
    graph_sink,
    graph_count,
    pair_list,
):
    sinks, evecs, _ = sink_slabs.shape
    graphs = graph_slot.shape[1]
    vmem = pl.BlockSpec(memory_space=pltpu.VMEM)
    hbm = pl.BlockSpec(memory_space=pl.ANY)
    smem = pl.BlockSpec(memory_space=pltpu.SMEM)
    slab = (evecs, evecs)
    edges = pl.pallas_call(
        functools.partial(fused_kernel, n, graphs),
        out_shape=jax.ShapeDtypeStruct((n, *slab), jnp.bfloat16),
        in_specs=[smem, smem, smem, smem, hbm, hbm, hbm],
        out_specs=vmem,
        scratch_shapes=[
            pltpu.VMEM((n, *slab), jnp.bfloat16),
            pltpu.VMEM((n, *slab), jnp.bfloat16),
            pltpu.VMEM((n * sinks + 1, *slab), jnp.bfloat16),
            pltpu.SMEM((2 * graphs,), jnp.int32),
            pltpu.VMEM(perambulators.shape, jnp.bfloat16),
            pltpu.VMEM(source_slabs.shape, jnp.bfloat16),
            pltpu.VMEM(sink_slabs.shape, jnp.bfloat16),
            pltpu.SemaphoreType.DMA((3,)),
            pltpu.SemaphoreType.DMA((n,)),
            pltpu.SemaphoreType.DMA((n,)),
            pltpu.SemaphoreType.DMA((3, n)),
            pltpu.SemaphoreType.DMA((n,)),
        ],
        compiler_params=pltpu.CompilerParams(collective_id=0, has_side_effects=True),
        name="contraction",
    )(
        send_pick,
        graph_slot[0].T,
        graph_sink[0].T,
        graph_count,
        perambulators,
        source_slabs,
        sink_slabs,
    )
    return pl.pallas_call(
        pair_kernel,
        out_shape=(
            jax.ShapeDtypeStruct((1, *slab), jnp.bfloat16),
            jax.ShapeDtypeStruct((pair_list.shape[0], *slab), jnp.bfloat16),
        ),
        in_specs=[smem, vmem],
        out_specs=(vmem, vmem),
        name="pairs",
    )(pair_list.T, edges)


def shards(readers, source_slabs, sink_slabs, perambulators, *tables):
    slabs = sink_slabs.shape[0]
    graphs = tables[1].shape[1]
    power = readers & (readers - 1) == 0 and readers % 4 == 0
    if power and readers * slabs <= 2 * graphs and graphs % UNROLL == 0 and slabs % 4 == 0:
        return fused_shards(readers, source_slabs, sink_slabs, perambulators, *tables)
    return looped_shards(source_slabs, sink_slabs, perambulators, *tables)


def solution(mesh):
    return jax.shard_map(
        functools.partial(shards, mesh.shape["had"]),
        mesh=mesh,
        in_specs=(
            P(("grp", "had"), None, None),
            P(("grp", "had"), None, None),
            P("grp", None, None, None),
            P(("grp", "had"), None),
            P(("grp", "had"), None, None),
            P(("grp", "had"), None, None),
            P(("grp", "had")),
            P(("grp", "had"), None),
        ),
        out_specs=(P(("grp", "had"), None, None), P(("grp", "had"), None, None)),
        check_vma=False,
    )
```
